32 devices in a mesh: sec: 8 (over y, x, core), blk: 4 (over z).
Axes of the slice: x: 2, y: 2, z: 4, core: 2. Of those that a mesh axis runs over, the one named last changes fastest.
Arguments:
- two_site: bfloat16 [256, 768, 768], P('sec', 'blk'), may hold values from -6 to 6
- left_env: bfloat16 [8, 768, 768], P('sec', 'blk'), may hold values from -0.21875 to 0.21875
- right_env: bfloat16 [8, 768, 768], P('sec', 'blk'), may hold values from -0.21875 to 0.21875
- left_size: int32 [8], replicated, may hold values from 1 to 768, 4608 in all
- right_size: int32 [8], replicated, may hold values from 1 to 768, 4608 in all
Outputs:
- gram: float32 [8, 768, 768], P('sec', 'blk')
The draws below stay inside these ranges and needn't reach their ends.
All inputs are finite; a program needn't handle non-finite values.
Results may differ from the reference program's by a relative error of at most 0.00096.
Values may be sent and summed in bfloat16 or wider, within the bound.
No kernel may reach another device: no remote copies, remote signals or barrier semaphores. Data moves between devices by JAX's collectives and lax.ppermute only.
A program may use at most 64 MiB of HBM per device.

```python
import math
import jax
import jax.numpy as jnp
import numpy as np
from jax import lax

M = 768
STATES = 2
PAIR_DEV = 32
NSEC = 8
NPAIR = 256


def block_levels(key, dims, pieces, smallest, largest):
    def one(dim, blocks):
        heights = jax.random.uniform(jax.random.fold_in(jax.random.fold_in(key, 6), dim), (blocks,), jnp.float32, smallest / len(pieces), largest / len(pieces))
        return jnp.repeat(jnp.exp(heights), dims[dim] // blocks).reshape((-1,) + (1,) * (len(dims) - dim - 1))

    loudness = one(*pieces[0])
    for cut in pieces[1:]:
        loudness = loudness * one(*cut)
    return loudness


def split_up(count, total, bound, skew):
    weights = [(1 << 20) // math.isqrt(standing ** skew) + 1 for standing in range(2, count + 1)]
    spare, holding = total - bound - (count - 1), [1] * (count - 1)
    while spare > 0:
        candidates = [i for i in range(count - 1) if holding[i] < bound]
        pool, remaining = sum([weights[i] for i in candidates]), spare
        for i in candidates:
            extra = min(bound - holding[i], max(1, remaining * weights[i] // pool), spare)
            holding[i] = holding[i] + extra
            spare = spare - extra
    return np.array([bound] + holding)


def ragged_sizes(own_key, number_of, total, most, skew):
    if number_of == 2:
        one = jax.random.randint(own_key, (), max(1, total - most), min(most, total - 1) + 1)
        return jnp.stack([one, total - one])
    sizes = jnp.asarray(split_up(number_of, total, most, skew), jnp.int32)
    couples = (number_of - 1) // 2
    source_of, sink = sizes[1:1 + 2 * couples:2], sizes[2:2 + 2 * couples:2]
    room = jnp.minimum(source_of - 1, most - sink)
    shifted = jax.random.randint(jax.random.fold_in(own_key, 1), (couples,), 0, 1 << 20) % (room + 1)
    sizes = sizes.at[1:1 + 2 * couples:2].set(source_of - shifted).at[2:2 + 2 * couples:2].set(sink + shifted)
    return sizes[jax.random.permutation(jax.random.fold_in(own_key, 2), number_of)]


def centred(key, extent, width, most, shards=(), kind=jnp.bfloat16):
    result = width * jax.random.normal(key, extent, jnp.float32)
    if shards:
        result = result * block_levels(key, extent, shards, -0.22, 0.18)
    return jnp.clip(result, -most, most).astype(kind)


def setup_inputs(seed: int = 0) -> dict:
    key_of = jax.random.split(jax.random.key(seed), 6)
    two_site = centred(key_of[0], (NPAIR, M, M), 1.0, 6.0, ((0, 8), (1, 4)))
    left_env = centred(key_of[1], (NSEC, M, M), M ** -0.5, 0.21875, ((0, 8), (1, 4)))
    right_env = centred(key_of[2], (NSEC, M, M), M ** -0.5, 0.21875, ((0, 8), (1, 4)))
    left_size = ragged_sizes(key_of[3], NSEC, NSEC * 3 * M // 4, M, 1).astype(jnp.int32)
    right_size = ragged_sizes(key_of[4], NSEC, NSEC * 3 * M // 4, M, 1).astype(jnp.int32)
    return dict(two_site=two_site, left_env=left_env, right_env=right_env, left_size=left_size, right_size=right_size)


def masked(envelope, live_size):
    index_row = jnp.arange(envelope.shape[1], dtype=jnp.int32)
    keep_live = (index_row[None, :, None] < live_size[:, None, None]) & (index_row[None, None, :] < live_size[:, None, None])
    return jnp.where(keep_live, envelope, jnp.zeros_like(envelope))


def reference(two_site, left_env, right_env, left_size, right_size):
    left_masked = masked(left_env, left_size)
    right_masked = masked(right_env, right_size)
    blocks = two_site.reshape(NSEC, PAIR_DEV, M, M)
    local_ids = jnp.arange(PAIR_DEV, dtype=jnp.int32)
    pair_ids = local_ids // STATES
    charge_first = (pair_ids // 4 + 1) // 2
    charge_second = (pair_ids % 4 + 1) // 2
    steps_right = charge_first + charge_second
    gram_scale = 1.0 / (8.0 * M)
    owner_ids = jnp.arange(NSEC, dtype=jnp.int32)

    def one_sector(running, items):
        left_block, block_group, sector_id = items
        right_index = ((sector_id + steps_right) % NSEC).astype(jnp.int32)
        chosen = jnp.take(right_masked, right_index, axis=0)
        left_half = jnp.einsum("km,pmn->pkn", left_block.astype(jnp.float32), block_group.astype(jnp.float32)).astype(jnp.bfloat16)
        applied = jnp.einsum("pkn,pcn->pkc", left_half.astype(jnp.float32), chosen.astype(jnp.float32)).astype(jnp.bfloat16)
        applied_wide = applied.astype(jnp.float32)
        squares = jnp.einsum("pkc,pkd->pcd", applied_wide, applied_wide)
        target = ((sector_id + charge_first) % NSEC).astype(jnp.int32)
        routing = (target[:, None] == owner_ids[None, :]).astype(jnp.float32)
        return running + gram_scale * jnp.einsum("po,pcd->ocd", routing, squares), None

    initial = jnp.zeros((NSEC, M, M), jnp.float32)
    gram, _ = lax.scan(one_sector, initial, (left_masked, blocks, owner_ids))
    return gram
```

```python
import jax
import jax.numpy as jnp
from jax import lax
from jax.sharding import PartitionSpec as P

STATES = 2
PAIRS = 16


def charge(level):
    return (level + 1) // 2


def rotate(block, axis, distance):
    size = lax.axis_size(axis)
    return lax.ppermute(block, axis, [(i, (i + distance) % size) for i in range(size)])


def pick_value(table, position):
    hits = jnp.arange(table.shape[0], dtype=jnp.int32) == position
    return jnp.sum(jnp.where(hits, table, jnp.zeros_like(table)))


def live_rows(block, live, first_row):
    rows, width = block.shape
    row_ids = first_row + jnp.arange(rows, dtype=jnp.int32)
    column_ids = jnp.arange(width, dtype=jnp.int32)
    keep = (row_ids[:, None] < live) & (column_ids[None, :] < live)
    return jnp.where(keep, block, jnp.zeros_like(block))


def body(two_site, left_env, right_env, left_size, right_size):
    sectors = lax.axis_size("sec")
    groups = lax.axis_size("blk")
    sec_index = lax.axis_index("sec")
    blk_index = lax.axis_index("blk")
    _, rows, width = two_site.shape
    pairs_here = PAIRS // groups
    behind = [(blk_index - s) % groups for s in range(groups)]
    ahead = [(blk_index + s) % groups for s in range(groups)]

    left_own = live_rows(left_env[0], pick_value(left_size, sec_index), blk_index * rows)
    left_parts = [rotate(left_own, "blk", s) if s else left_own for s in range(groups)]
    right_own = live_rows(right_env[0], pick_value(right_size, sec_index), blk_index * rows)
    right_parts = [rotate(right_own, "blk", s) if s else right_own for s in range(groups)]

    column_ids = jnp.arange(width, dtype=jnp.int32)
    arrival = (blk_index - column_ids // rows) % groups * rows + column_ids % rows
    reorder = (column_ids[:, None] == arrival[None, :]).astype(jnp.bfloat16)
    left_full = jnp.dot(
        jnp.concatenate(left_parts, axis=0), reorder, preferred_element_type=jnp.float32
    ).astype(jnp.bfloat16)

    right_full = jnp.stack(right_parts)
    right_full = jnp.take(right_full, jnp.stack(behind), axis=0).reshape(width, width)

    right_of = []
    arrived = {}
    for j in range(pairs_here):
        route = []
        for b in range(sectors):
            for z in range(groups):
                pair = z * pairs_here + j
                step = charge(pair // 4) + charge(pair % 4)
                route.append((b * groups + z, (b - step) % sectors * groups + z))
        key = tuple(route)
        if key not in arrived:
            arrived[key] = lax.ppermute(right_full, ("sec", "blk"), route)
        right_of.append(arrived[key])

    grouped = two_site.reshape(groups, pairs_here, STATES, rows, width)
    total = jnp.zeros((width, width), jnp.float32)
    for j in range(pairs_here):
        pieces = []
        for s in range(groups):
            piece = lax.dynamic_index_in_dim(grouped[:, j], ahead[s], 0, keepdims=False)
            pieces.append(rotate(piece, "blk", s) if s else piece)
        block = jnp.concatenate(pieces, axis=1)
        half = jnp.einsum(
            "km,smn->skn", left_full, block, preferred_element_type=jnp.float32
        ).astype(jnp.bfloat16)
        applied = jnp.einsum(
            "skn,cn->skc", half, right_of[j], preferred_element_type=jnp.float32
        ).astype(jnp.bfloat16)
        applied = applied.reshape(STATES * width, width)
        total = total + lax.dot_general(
            applied, applied, (((0,), (0,)), ((), ())), preferred_element_type=jnp.float32
        )
    total = (total * (1.0 / (8.0 * width))).reshape(groups, rows, width)

    sums = [jnp.zeros((rows, width), jnp.float32) for _ in range(3)]
    for s in range(groups):
        part = lax.dynamic_index_in_dim(total, ahead[s], 0, keepdims=False)
        part = rotate(part, "blk", s) if s else part
        came_up = charge(behind[s] * pairs_here // 4)
        for q in range(3):
            sums[q] = sums[q] + jnp.where(came_up == q, part, jnp.zeros_like(part))
    gram_rows = sums[0] + rotate(sums[1], "sec", 1) + rotate(sums[2], "sec", 2)
    return gram_rows[None]


def solution(mesh):
    placed = (P("sec", "blk", None), P("sec", "blk", None), P("sec", "blk", None), P(), P())
    return jax.shard_map(
        body, mesh=mesh, in_specs=placed, out_specs=P("sec", "blk", None), check_vma=False
    )
```

```python
import functools
import jax
import jax.numpy as jnp
from jax import lax
from jax.experimental import pallas as pl
from jax.experimental.pallas import tpu as pltpu
from jax.sharding import PartitionSpec as P

STATES = 2
PAIRS = 16
PAD = 16
WINDOW = 3


def charge(level):
    return (level + 1) // 2


def rotate(block, axis, distance):
    size = lax.axis_size(axis)
    return lax.ppermute(block, axis, [(i, (i + distance) % size) for i in range(size)])


def pick_value(table, position):
    hits = jnp.arange(table.shape[0], dtype=jnp.int32) == position
    return jnp.sum(jnp.where(hits, table, jnp.zeros_like(table)))


def live_rows(block, live, first_row):
    rows, width = block.shape
    row_ids = first_row + jnp.arange(rows, dtype=jnp.int32)
    column_ids = jnp.arange(width, dtype=jnp.int32)
    keep = (row_ids[:, None] < live) & (column_ids[None, :] < live)
    return jnp.where(keep, block, jnp.zeros_like(block))


def block_kernel(groups, first, last, scale, where_ref, *refs):
    left_ref, right_ref = refs[:2]
    pieces = refs[2 : 2 + groups]
    rest = refs[2 + groups :]
    if not first:
        before_ref, rest = rest[0], rest[1:]
    if last:
        sends, (total_ref, block_ref) = rest[:groups], rest[groups:]
    else:
        total_ref, block_ref = rest
    rows = pieces[0].shape[-2]
    z = where_ref[0]
    for s in range(groups):
        start = pl.multiple_of(lax.rem(z + groups - s, groups) * rows, rows)
        block_ref[pl.ds(start, rows), :] = pieces[s][0]
    half = jnp.dot(
        left_ref[...], block_ref[...], preferred_element_type=jnp.float32
    ).astype(jnp.bfloat16)
    applied = lax.dot_general(
        right_ref[...], half, (((1,), (1,)), ((), ())), preferred_element_type=jnp.float32
    ).astype(jnp.bfloat16)
    square = lax.dot_general(
        applied, applied, (((1,), (1,)), ((), ())), preferred_element_type=jnp.float32
    )
    if first:
        total_ref[...] = square
    else:
        total_ref[...] = before_ref[...] + square
    if last:
        width = total_ref.shape[1]
        for s in range(groups):
            start = pl.multiple_of(lax.rem(z + s, groups) * rows, rows)
            part = scale * total_ref[pl.ds(start, rows), :]
            short = part.astype(jnp.bfloat16)
            row_ids = start + lax.broadcasted_iota(jnp.int32, (rows, width), 0)
            column_ids = lax.broadcasted_iota(jnp.int32, (rows, width), 1)
            gap = jnp.where(row_ids == column_ids, part - short.astype(jnp.float32), 0.0)
            gap = jnp.sum(gap, axis=0, keepdims=True)
            sends[s][:rows, :] = short
            sends[s][rows:, :] = jnp.broadcast_to(gap, (PAD, width)).astype(jnp.bfloat16)


def one_block(z, left, right, two_site, own_base, pieces, before, last, scale):
    groups = len(pieces) + 1
    rows, width = pieces[0].shape
    first = before is None
    whole = pl.BlockSpec((width, width), lambda i, w: (0, 0))
    piece_spec = pl.BlockSpec((1, rows, width), lambda i, w: (0, 0, 0))
    own_spec = pl.BlockSpec((1, rows, width), lambda i, w: (w[1], 0, 0))
    in_specs = [whole, whole, own_spec] + [piece_spec] * (groups - 1)
    operands = [left, right, two_site] + [p[None] for p in pieces]
    if not first:
        in_specs.append(whole)
        operands.append(before)
    scratch = [pltpu.VMEM((width, width), jnp.bfloat16)]
    if last:
        out_shape = [jax.ShapeDtypeStruct((rows + PAD, width), jnp.bfloat16)] * groups
        out_specs = [pl.BlockSpec((rows + PAD, width), lambda i, w: (0, 0))] * groups
        scratch = [pltpu.VMEM((width, width), jnp.float32)] + scratch
        aliases = {}
    else:
        out_shape = jax.ShapeDtypeStruct((width, width), jnp.float32)
        out_specs = whole
        aliases = {} if first else {len(operands): 0}
    return pl.pallas_call(
        functools.partial(block_kernel, groups, first, last, scale),
        out_shape=out_shape,
        grid_spec=pltpu.PrefetchScalarGridSpec(
            num_scalar_prefetch=1, grid=(1,), in_specs=in_specs, out_specs=out_specs,
            scratch_shapes=scratch,
        ),
        input_output_aliases=aliases,
        cost_estimate=pl.CostEstimate(
            flops=6 * width**3, transcendentals=0, bytes_accessed=12 * width * width
        ),
        name="last_block" if last else "one_block",
    )(jnp.stack([z, own_base]), *operands)


def named(block, distance):
    if not distance:
        return block
    return rotate(block, "blk", distance)


def body(two_site, left_env, right_env, left_size, right_size):
    sectors = lax.axis_size("sec")
    groups = lax.axis_size("blk")
    sec_index = lax.axis_index("sec")
    blk_index = lax.axis_index("blk")
    total_blocks, rows, width = two_site.shape
    pairs_here = PAIRS // groups
    here = total_blocks // groups
    behind = [(blk_index - s) % groups for s in range(groups)]
    ahead = [(blk_index + s) % groups for s in range(groups)]

    left_own = live_rows(left_env[0], pick_value(left_size, sec_index), blk_index * rows)
    left_parts = [named(left_own, s) for s in range(groups)]
    right_own = live_rows(right_env[0], pick_value(right_size, sec_index), blk_index * rows)
    right_parts = [named(right_own, s) for s in range(groups)]
    left_full = jnp.concatenate(left_parts, axis=0)
    right_full = jnp.take(jnp.stack(right_parts), jnp.stack(behind), axis=0)
    right_full = right_full.reshape(width, width)

    right_of = []
    arrived = {}
    for j in range(pairs_here):
        route = []
        for b in range(sectors):
            for z in range(groups):
                pair = z * pairs_here + j
                step = charge(pair // 4) + charge(pair % 4)
                route.append((b * groups + z, (b - step) % sectors * groups + z))
        key = tuple(route)
        if key not in arrived:
            arrived[key] = lax.ppermute(right_full, ("sec", "blk"), route)
        right_of.append(arrived[key])

    totals = []
    for c in range(here):
        pieces = [
            lax.dynamic_index_in_dim(two_site, ahead[s] * here + c, 0, keepdims=False)
            for s in range(1, groups)
        ]
        if c >= WINDOW:
            pieces, totals[c - WINDOW] = lax.optimization_barrier((pieces, totals[c - WINDOW]))
        pieces = [named(p, s + 1) for s, p in enumerate(pieces)]
        totals.append(
            one_block(
                blk_index, left_full, right_of[c // STATES], two_site, blk_index * here + c,
                pieces, totals[-1] if c else None, c == here - 1, 1.0 / (8.0 * width),
            )
        )
    total = totals[-1]

    gram_rows = jnp.zeros((rows, width), jnp.float32)
    row_ids = blk_index * rows + jnp.arange(rows, dtype=jnp.int32)
    on_diagonal = row_ids[:, None] == jnp.arange(width, dtype=jnp.int32)[None, :]
    for s in range(groups):
        route = []
        for b in range(sectors):
            for z in range(groups):
                up = charge(z * pairs_here // 4)
                route.append((b * groups + z, (b + up) % sectors * groups + (z + s) % groups))
        part = lax.ppermute(total[s], ("sec", "blk"), route).astype(jnp.float32)
        gram_rows = gram_rows + part[:rows] + jnp.where(on_diagonal, part[rows][None, :], 0.0)
    return gram_rows[None]


def solution(mesh):
    placed = (P("sec", "blk", None), P("sec", "blk", None), P("sec", "blk", None), P(), P())
    return jax.shard_map(
        body, mesh=mesh, in_specs=placed, out_specs=P("sec", "blk", None), check_vma=False
    )
```

```python
import functools
import jax
import jax.numpy as jnp
from jax import lax
from jax.experimental import pallas as pl
from jax.experimental.pallas import tpu as pltpu
from jax.sharding import PartitionSpec as P

STATES = 2
PAIRS = 16
PAD = 16
WINDOW = 5


def charge(level):
    return (level + 1) // 2


def rotate(block, axis, distance):
    size = lax.axis_size(axis)
    return lax.ppermute(block, axis, [(i, (i + distance) % size) for i in range(size)])


def pick_value(table, position):
    hits = jnp.arange(table.shape[0], dtype=jnp.int32) == position
    return jnp.sum(jnp.where(hits, table, jnp.zeros_like(table)))


def live_rows(block, live, first_row):
    rows, width = block.shape
    row_ids = first_row + jnp.arange(rows, dtype=jnp.int32)
    column_ids = jnp.arange(width, dtype=jnp.int32)
    keep = (row_ids[:, None] < live) & (column_ids[None, :] < live)
    return jnp.where(keep, block, jnp.zeros_like(block))


def block_kernel(groups, first, last, scale, where_ref, *refs):
    left_ref, right_ref = refs[:2]
    pieces = refs[2 : 2 + groups]
    rest = refs[2 + groups :]
    if not first:
        before_ref, rest = rest[0], rest[1:]
    if last:
        sends, (total_ref, block_ref) = rest[:groups], rest[groups:]
    else:
        total_ref, block_ref = rest
    rows = pieces[0].shape[-2]
    z = where_ref[0]
    for s in range(groups):
        start = pl.multiple_of(lax.rem(z + groups - s, groups) * rows, rows)
        block_ref[pl.ds(start, rows), :] = pieces[s][0]
    half = jnp.dot(
        left_ref[...], block_ref[...], preferred_element_type=jnp.float32
    ).astype(jnp.bfloat16)
    applied = lax.dot_general(
        right_ref[...], half, (((1,), (1,)), ((), ())), preferred_element_type=jnp.float32
    ).astype(jnp.bfloat16)
    square = lax.dot_general(
        applied, applied, (((1,), (1,)), ((), ())), preferred_element_type=jnp.float32
    )
    if first:
        total_ref[...] = square
    else:
        total_ref[...] = before_ref[...] + square
    if last:
        width = total_ref.shape[1]
        for s in range(groups):
            start = pl.multiple_of(lax.rem(z + s, groups) * rows, rows)
            part = scale * total_ref[pl.ds(start, rows), :]
            short = part.astype(jnp.bfloat16)
            row_ids = start + lax.broadcasted_iota(jnp.int32, (rows, width), 0)
            column_ids = lax.broadcasted_iota(jnp.int32, (rows, width), 1)
            gap = jnp.where(row_ids == column_ids, part - short.astype(jnp.float32), 0.0)
            gap = jnp.sum(gap, axis=0, keepdims=True)
            sends[s][:rows, :] = short
            sends[s][rows:, :] = jnp.broadcast_to(gap, (PAD, width)).astype(jnp.bfloat16)


def one_block(z, left, right, two_site, c, here, pieces, before, last, scale):
    groups = len(pieces) + 1
    rows, width = pieces[0].shape
    first = before is None
    whole = pl.BlockSpec((width, width), lambda i, w: (0, 0))
    piece_spec = pl.BlockSpec((1, rows, width), lambda i, w: (0, 0, 0))
    own_spec = pl.BlockSpec((1, rows, width), lambda i, w: (w[0] * here + c, 0, 0))
    in_specs = [whole, whole, own_spec] + [piece_spec] * (groups - 1)
    operands = [left, right, two_site] + [p[None] for p in pieces]
    if not first:
        in_specs.append(whole)
        operands.append(before)
    scratch = [pltpu.VMEM((width, width), jnp.bfloat16)]
    if last:
        out_shape = [jax.ShapeDtypeStruct((rows + PAD, width), jnp.bfloat16)] * groups
        out_specs = [pl.BlockSpec((rows + PAD, width), lambda i, w: (0, 0))] * groups
        scratch = [pltpu.VMEM((width, width), jnp.float32)] + scratch
        aliases = {}
    else:
        out_shape = jax.ShapeDtypeStruct((width, width), jnp.float32)
        out_specs = whole
        aliases = {} if first else {len(operands): 0}
    return pl.pallas_call(
        functools.partial(block_kernel, groups, first, last, scale),
        out_shape=out_shape,
        grid_spec=pltpu.PrefetchScalarGridSpec(
            num_scalar_prefetch=1, grid=(1,), in_specs=in_specs, out_specs=out_specs,
            scratch_shapes=scratch,
        ),
        input_output_aliases=aliases,
        cost_estimate=pl.CostEstimate(
            flops=6 * width**3, transcendentals=0, bytes_accessed=12 * width * width
        ),
        name="last_block" if last else "one_block",
    )(z.astype(jnp.int32)[None], *operands)


def named(block, distance):
    return rotate(block, "blk", distance)


def forward(block, step, up):
    last = lax.axis_size("blk") - 1
    route = [(i, i + 1) for i in range(step - 1, last)]
    if not up:
        route = [(last - i, last - j) for i, j in route]
    return lax.ppermute(block, "blk", route)


def in_order(from_below, from_above, blk_index):
    rows, width = from_below[0].shape
    groups = len(from_below)
    line = jnp.concatenate(from_below[:0:-1] + from_above, axis=0)
    return lax.dynamic_slice(line, ((groups - 1 - blk_index) * rows, 0), (groups * rows, width))


def body(two_site, left_env, right_env, left_size, right_size):
    sectors = lax.axis_size("sec")
    groups = lax.axis_size("blk")
    sec_index = lax.axis_index("sec")
    blk_index = lax.axis_index("blk")
    total_blocks, rows, width = two_site.shape
    pairs_here = PAIRS // groups
    here = total_blocks // groups
    ahead = [(blk_index + s) % groups for s in range(groups)]

    right_own = live_rows(right_env[0], pick_value(right_size, sec_index), blk_index * rows)
    left_own = live_rows(left_env[0], pick_value(left_size, sec_index), blk_index * rows)
    right_up, right_down = [right_own], [right_own]
    left_up, left_down = [left_own], [left_own]

    def send(c, *after):
        pieces = [
            lax.dynamic_index_in_dim(two_site, ahead[s] * here + c, 0, keepdims=False)
            for s in range(1, groups)
        ]
        if after:
            pieces, after = lax.optimization_barrier((pieces, after))
        return [named(p, s + 1) for s, p in enumerate(pieces)], after

    chunks = []
    for t in range(groups):
        if t < groups - 1:
            right_up.append(forward(right_up[t], t + 1, True))
            right_down.append(forward(right_down[t], t + 1, False))
        if t:
            left_up.append(forward(left_up[t - 1], t, True))
            left_down.append(forward(left_down[t - 1], t, False))
        if t < here:
            if t:
                sent, (right_up[t], right_down[t]) = send(t, right_up[t], right_down[t])
            else:
                sent, _ = send(t)
            chunks.append(sent)
    right_full = in_order(right_up, right_down, blk_index)
    if here > groups:
        last = groups - 1
        sent, (left_up[last], left_down[last]) = send(groups, left_up[last], left_down[last])
        chunks.append(sent)
    left_full = in_order(left_up, left_down, blk_index)

    right_of = []
    arrived = {}
    for j in range(pairs_here):
        route = []
        for b in range(sectors):
            for z in range(groups):
                pair = z * pairs_here + j
                step = charge(pair // 4) + charge(pair % 4)
                route.append((b * groups + z, (b - step) % sectors * groups + z))
        key = tuple(route)
        if key not in arrived:
            arrived[key] = lax.ppermute(right_full, ("sec", "blk"), route)
        right_of.append(arrived[key])

    totals = []
    for c in range(here):
        if c >= len(chunks):
            sent, (totals[c - WINDOW],) = send(c, totals[c - WINDOW])
            chunks.append(sent)
        totals.append(
            one_block(
                blk_index, left_full, right_of[c // STATES], two_site, c, here,
                chunks[c], totals[-1] if c else None, c == here - 1, 1.0 / (8.0 * width),
            )
        )
    total = totals[-1]

    gram_rows = jnp.zeros((rows, width), jnp.float32)
    row_ids = blk_index * rows + jnp.arange(rows, dtype=jnp.int32)
    on_diagonal = row_ids[:, None] == jnp.arange(width, dtype=jnp.int32)[None, :]
    for s in range(groups):
        route = []
        for b in range(sectors):
            for z in range(groups):
                up = charge(z * pairs_here // 4)
                route.append((b * groups + z, (b + up) % sectors * groups + (z + s) % groups))
        part = lax.ppermute(total[s], ("sec", "blk"), route).astype(jnp.float32)
        gram_rows = gram_rows + part[:rows] + jnp.where(on_diagonal, part[rows][None, :], 0.0)
    return gram_rows[None]


def solution(mesh):
    placed = (P("sec", "blk", None), P("sec", "blk", None), P("sec", "blk", None), P(), P())
    return jax.shard_map(
        body, mesh=mesh, in_specs=placed, out_specs=P("sec", "blk", None), check_vma=False
    )
```
